256 devices in a mesh: docs: 8 (over x, core), seq: 32 (over z, y).
Axes of the slice: x: 4, y: 4, z: 8, core: 2. Of those that a mesh axis runs over, the one named last changes fastest.
Arguments:
- byte_input: bfloat16 [81920, 256], P(('docs', 'seq')), parts along dimension 0, may hold values from -6 to 6
- w_short: bfloat16 [1024, 1024], replicated, may hold values from -0.1875 to 0.1875
- w_attend: bfloat16 [1024, 3072], replicated, may hold values from -0.1875 to 0.1875
- w_expand: bfloat16 [1024, 1024], replicated, may hold values from -0.75 to 0.75
- out_grad: bfloat16 [81920, 256], P(('docs', 'seq')), parts along dimension 0, may hold values from -6 to 6
Outputs:
- byte_output: bfloat16 [81920, 256], P(('docs', 'seq')), parts along dimension 0
- input_grad: bfloat16 [81920, 256], P(('docs', 'seq')), parts along dimension 0
- grad_short: float32 [8192, 1024], P(('docs', 'seq')), parts along dimension 0
- grad_attend: float32 [8192, 3072], P(('docs', 'seq')), parts along dimension 0
- grad_expand: float32 [8192, 1024], P(('docs', 'seq')), parts along dimension 0
The draws below stay inside these ranges and needn't reach their ends.
There are 8 independent parts, one for each index of `docs`. The reference program is written for one: setup_inputs(seed, part) draws one part's arguments, and reference() takes and returns one part's arrays. A program takes and returns all parts, laid end to end along the dimension named above; an argument that names none is the same for every part. Nothing has to cross between parts.
All inputs are finite; a program needn't handle non-finite values.
Results may differ from the reference program's by a relative error of at most 0.028.
Values may be sent and summed in bfloat16 or wider, within the bound.
No kernel may reach another device: no remote copies, remote signals or barrier semaphores. Data moves between devices by JAX's collectives and lax.ppermute only.
A program may use at most 128 MiB of HBM per device.

```python
import jax
import jax.numpy as jnp
from jax import lax

E = 256
D = 1024
HEADS = 8
DH = 128
A = 1024
T_DEV = 80
SHORT = 2560
BYTES = 10240
N_SEQ = 32


def steps_of(stream_key, shape, cuts, smallest, high):
    level, own = 1.0, jax.random.fold_in(stream_key, 6)
    for dim, shards_of in cuts:
        steps = jnp.exp(jax.random.uniform(jax.random.fold_in(own, dim), (shards_of,), jnp.float32, smallest / len(cuts), high / len(cuts)))
        level = level * jnp.repeat(steps, shape[dim] // shards_of).reshape([-1 if axis == dim else 1 for axis in range(len(shape))])
    return level


def noise(stream_key, extent, width, most, pieces=(), kind=jnp.bfloat16):
    entries = jax.random.normal(stream_key, extent, jnp.float32) * width
    if len(pieces) > 0:
        entries = steps_of(stream_key, extent, pieces, -0.22, 0.18) * entries
    return jnp.clip(entries, min=-most, max=most).astype(kind)


def setup_inputs(seed: int = 0, part: int = 0) -> dict:
    key_of = jax.random.split(jax.random.key(seed), 6)
    part_splits = jax.random.split(jax.random.fold_in(key_of[5], part), 6)
    byte_input = noise(part_splits[0], (BYTES, E), 1.0, 6.0, ((0, 32),))
    w_short = noise(key_of[1], (4 * E, D), (4 * E) ** -0.5, 0.1875)
    w_attend = noise(key_of[2], (D, 3 * A), D ** -0.5, 0.1875)
    w_expand = noise(key_of[3], (A, 4 * E), (A // 16) ** -0.5, 0.75)
    out_grad = noise(part_splits[4], (BYTES, E), 1.0, 6.0, ((0, 32),))
    return {"byte_input": byte_input, "w_short": w_short, "w_attend": w_attend, "w_expand": w_expand, "out_grad": out_grad}


SCORE_BOUND = 16.0
EPSILON = 1e-06

def rounded(value):
    return lax.optimization_barrier(value.astype(jnp.bfloat16))

def unit_heads(matrix):
    split = matrix.reshape(matrix.shape[0], HEADS, -1)
    scale = lax.rsqrt(lax.optimization_barrier(jnp.mean(split * split, axis=2, keepdims=True)) + EPSILON)
    return (split * scale, scale)

def norm_back(normed, scale, upstream):
    inner = lax.optimization_barrier(jnp.mean(normed * upstream, axis=2, keepdims=True))
    return scale * (upstream - normed * inner)

def powers_of(query_f, key_f, query_pos, key_pos):
    dots = jnp.einsum('thd,rhd->htr', query_f, key_f)
    live = query_pos[:, None] >= key_pos[None, :]
    return jnp.where(live[None], jnp.exp(dots * (SCORE_BOUND / DH)), 0.0)

def reference(byte_input, w_short, w_attend, w_expand, out_grad):
    shifted = jnp.concatenate([jnp.zeros((3, E), byte_input.dtype), byte_input[:-3]], axis=0)
    grouped = shifted.reshape(SHORT, 4 * E)
    hidden = jnp.dot(grouped, w_short, preferred_element_type=jnp.float32)
    hidden_scale = lax.rsqrt(lax.optimization_barrier(jnp.mean(hidden * hidden, axis=1, keepdims=True)) + EPSILON)
    normed = hidden * hidden_scale
    normed_b = normed.astype(jnp.bfloat16)
    projected = jnp.dot(normed_b, w_attend, preferred_element_type=jnp.float32)
    query_unit, query_scale = unit_heads(projected[:, :A])
    key_unit, key_scale = unit_heads(projected[:, A:2 * A])
    query_f = rounded(query_unit).astype(jnp.float32)
    key_f = rounded(key_unit).astype(jnp.float32)
    value_f = rounded(projected[:, 2 * A:]).astype(jnp.float32).reshape(SHORT, HEADS, DH)
    positions = jnp.arange(SHORT, dtype=jnp.int32)

    def forward_block(number):
        offset = number * T_DEV
        query_pos = offset + jnp.arange(T_DEV, dtype=jnp.int32)
        block_query = lax.dynamic_slice_in_dim(query_f, offset, T_DEV, 0)
        powers = powers_of(block_query, key_f, query_pos, positions)
        weighted = jnp.einsum('htr,rhd->thd', rounded(powers).astype(jnp.float32), value_f)
        return (weighted, lax.optimization_barrier(jnp.sum(powers, axis=2)).T)
    weighted, denom = lax.map(forward_block, jnp.arange(N_SEQ, dtype=jnp.int32))
    weighted = weighted.reshape(SHORT, HEADS, DH)
    denom = denom.reshape(SHORT, HEADS)
    attended = rounded((weighted / denom[:, :, None]).reshape(SHORT, A))
    expanded = jnp.dot(attended, w_expand, preferred_element_type=jnp.float32)
    byte_output = (byte_input.astype(jnp.float32) + expanded.reshape(BYTES, E)).astype(jnp.bfloat16)
    d_expand = out_grad.reshape(SHORT, 4 * E)
    d_attended = rounded(jnp.dot(d_expand, w_expand.T, preferred_element_type=jnp.float32))
    d_attended = d_attended.astype(jnp.float32).reshape(SHORT, HEADS, DH)
    inverse = 1.0 / denom
    grad_scaled = rounded(d_attended * inverse[:, :, None]).astype(jnp.float32)
    attended_f = attended.astype(jnp.float32).reshape(SHORT, HEADS, DH)
    shift_term = rounded(lax.optimization_barrier(jnp.sum(d_attended * attended_f, axis=2)) * inverse).astype(jnp.float32)

    def backward_block(totals, number):
        key_total, value_total = totals
        offset = number * T_DEV
        query_pos = offset + jnp.arange(T_DEV, dtype=jnp.int32)
        block_query = lax.dynamic_slice_in_dim(query_f, offset, T_DEV, 0)
        block_grad = lax.dynamic_slice_in_dim(grad_scaled, offset, T_DEV, 0)
        block_shift = lax.dynamic_slice_in_dim(shift_term, offset, T_DEV, 0)
        powers = powers_of(block_query, key_f, query_pos, positions)
        grad_dot = jnp.einsum('thd,rhd->htr', block_grad, value_f)
        d_score = rounded(powers * (grad_dot - block_shift.T[:, :, None]) * (SCORE_BOUND / DH)).astype(jnp.float32)
        query_part = jnp.einsum('htr,rhd->thd', d_score, key_f)
        key_part = jnp.einsum('htr,thd->rhd', d_score, block_query)
        value_part = jnp.einsum('htr,thd->rhd', rounded(powers).astype(jnp.float32), block_grad)
        key_total = key_total + rounded(key_part).astype(jnp.float32)
        value_total = value_total + rounded(value_part).astype(jnp.float32)
        return ((key_total, value_total), query_part)
    zero_heads = jnp.zeros((SHORT, HEADS, DH), jnp.float32)
    (key_grad, value_grad), query_grad = lax.scan(backward_block, (zero_heads, zero_heads), jnp.arange(N_SEQ, dtype=jnp.int32))
    query_grad = query_grad.reshape(SHORT, HEADS, DH)
    d_query = norm_back(query_unit, query_scale, query_grad).reshape(SHORT, A)
    d_key = norm_back(key_unit, key_scale, key_grad).reshape(SHORT, A)
    d_projected = jnp.concatenate([d_query, d_key, value_grad.reshape(SHORT, A)], axis=1).astype(jnp.bfloat16)
    d_normed = jnp.dot(d_projected, w_attend.T, preferred_element_type=jnp.float32)
    d_hidden = (hidden_scale * (d_normed - normed * lax.optimization_barrier(jnp.mean(normed * d_normed, axis=1, keepdims=True)))).astype(jnp.bfloat16)
    d_grouped = rounded(jnp.dot(d_hidden, w_short.T, preferred_element_type=jnp.float32))
    flat = d_grouped.reshape(BYTES, E).astype(jnp.float32)
    moved = jnp.concatenate([flat[3:], jnp.zeros((3, E), jnp.float32)], axis=0)
    input_grad = (out_grad.astype(jnp.float32) + moved).astype(jnp.bfloat16)

    def grad_block(totals, number):
        offset = number * T_DEV

        def part(left, right):
            left_rows = lax.dynamic_slice_in_dim(left, offset, T_DEV, 0)
            right_rows = lax.dynamic_slice_in_dim(right, offset, T_DEV, 0)
            return rounded(jnp.dot(left_rows.T, right_rows, preferred_element_type=jnp.float32)).astype(jnp.float32)
        return ((totals[0] + part(grouped, d_hidden), totals[1] + part(normed_b, d_projected), totals[2] + part(attended, d_expand)), None)
    start_grads = (jnp.zeros((4 * E, D), jnp.float32), jnp.zeros((D, 3 * A), jnp.float32), jnp.zeros((A, 4 * E), jnp.float32))
    grads, unused = lax.scan(grad_block, start_grads, jnp.arange(N_SEQ, dtype=jnp.int32))
    return (byte_output, input_grad, grads[0], grads[1], grads[2])
```

```python
import functools

import jax
import jax.numpy as jnp
from jax import lax
from jax.experimental import pallas as pl
from jax.experimental.pallas import tpu as pltpu
from jax.sharding import Mesh, PartitionSpec as P

HEADS = 8


SCORE_BOUND = 16.0
EPSILON = 1e-06

NT = (((1,), (1,)), ((), ()))
TN = (((0,), (0,)), ((), ()))


def mm(left, right, dims=(((1,), (0,)), ((), ()))):
    return lax.dot_general(left, right, dims, preferred_element_type=jnp.float32)


def unit(matrix):
    scale = lax.rsqrt(jnp.mean(matrix * matrix, axis=1, keepdims=True) + EPSILON)
    return (matrix * scale, scale)


def norm_back(normed, scale, upstream):
    inner = jnp.mean(normed * upstream, axis=1, keepdims=True)
    return scale * (upstream - normed * inner)


def chunks_of(rows, block, width=256):
    found = []
    for first in range(0, rows, width):
        found.append((first, min(width, rows - first), first // block * block))
    return found


def attention_body(block, shards, y_ref, qd_ref, *refs):
    kv_refs = refs[:shards]
    att_ref, dq_ref, own_ref = refs[shards : shards + 3]
    sent_refs = refs[shards + 3 : 2 * shards + 2]
    p_ref, kb_ref, acc_ref, dq_acc = refs[2 * shards + 2 :]
    rows, head_size = att_ref.shape
    factor = SCORE_BOUND / head_size
    chunks = chunks_of(rows, block)
    y = y_ref[0]
    query_unit, query_scale = unit(qd_ref[:, :head_size].astype(jnp.float32))
    qb = query_unit.astype(jnp.bfloat16)
    qpos = lax.broadcasted_iota(jnp.int32, (rows, 1), 0)
    start = jnp.zeros((rows, 1), jnp.int32)
    for edge in range(block, rows, block):
        start = start + jnp.where(qpos >= edge, block, 0)
    denom = jnp.zeros((rows, 1), jnp.float32)
    acc_ref[...] = jnp.zeros_like(acc_ref)
    for turn in range(shards):
        key_unit, _ = unit(kv_refs[turn][:, :head_size].astype(jnp.float32))
        kb_ref[turn] = key_unit.astype(jnp.bfloat16)
        limit = qpos + 1 if turn == 0 else start + jnp.where(y >= turn, block, 0)
        for number, (first, width, row) in enumerate(chunks):
            dots = mm(qb[row:], kb_ref[turn, first : first + width], NT)
            key_pos = first + lax.broadcasted_iota(jnp.int32, (rows - row, width), 1)
            powers = jnp.where(key_pos < limit[row:], jnp.exp(dots * factor), 0.0)
            p_ref[turn, number, row:, :width] = powers
            part = jnp.sum(powers, axis=1, keepdims=True)
            denom = denom + (part if row == 0 else jnp.concatenate([jnp.zeros((row, 1), jnp.float32), part], axis=0))
            acc_ref[row:] += mm(powers.astype(jnp.bfloat16), kv_refs[turn][first : first + width, head_size:])
    inverse = 1.0 / denom
    attended = (acc_ref[...] * inverse).astype(jnp.bfloat16)
    att_ref[...] = attended
    d_attended = qd_ref[:, head_size:].astype(jnp.float32)
    grad = (d_attended * inverse).astype(jnp.bfloat16)
    shift = jnp.sum(d_attended * attended.astype(jnp.float32), axis=1, keepdims=True) * inverse
    shift = shift.astype(jnp.bfloat16).astype(jnp.float32)
    dq_acc[...] = jnp.zeros_like(dq_acc)
    for turn in range(shards):
        out = own_ref if turn == 0 else sent_refs[turn - 1]
        for number, (first, width, row) in enumerate(chunks):
            powers = p_ref[turn, number, row:, :width]
            grad_dot = mm(grad[row:], kv_refs[turn][first : first + width, head_size:], NT)
            d_score = (powers * (grad_dot - shift[row:]) * factor).astype(jnp.bfloat16)
            dq_acc[row:] += mm(d_score, kb_ref[turn, first : first + width])
            out[first : first + width, :head_size] = mm(d_score, qb[row:], TN).astype(out.dtype)
            out[first : first + width, head_size:] = mm(powers.astype(jnp.bfloat16), grad[row:], TN).astype(out.dtype)
    dq_ref[...] = norm_back(query_unit, query_scale, dq_acc[...]).astype(jnp.bfloat16)


def attention(y, qd, kvs, block):
    rows, width = qd.shape
    head_size = width // 2
    shards = len(kvs)
    vmem = pl.BlockSpec(memory_space=pltpu.VMEM)
    shape = jax.ShapeDtypeStruct
    outs = [shape((rows, head_size), jnp.bfloat16)] * 2
    outs += [shape((rows, width), jnp.float32)] + [shape((rows, width), jnp.bfloat16)] * (shards - 1)
    return pl.pallas_call(
        functools.partial(attention_body, block, shards),
        out_shape=outs,
        in_specs=[pl.BlockSpec(memory_space=pltpu.SMEM)] + [vmem] * (shards + 1),
        out_specs=[vmem] * len(outs),
        scratch_shapes=[
            pltpu.VMEM((shards, len(chunks_of(rows, block)), rows, 256), jnp.float32),
            pltpu.VMEM((shards, rows, head_size), jnp.bfloat16),
            pltpu.VMEM((rows, head_size), jnp.float32),
            pltpu.VMEM((rows, head_size), jnp.float32),
        ],
        compiler_params=pltpu.CompilerParams(vmem_limit_bytes=40 * 1024 * 1024),
        name="attention",
    )(y, qd, *kvs)


def local(byte_input, w_short, w_attend, w_expand, out_grad):
    z_size, y_size = lax.axis_size("z"), lax.axis_size("y")
    count = z_size * y_size
    short_rows = byte_input.shape[0] // 4
    byte_width = byte_input.shape[1]
    attn_width = w_attend.shape[1] // 3
    model_width = w_short.shape[1]
    head_size = attn_width // HEADS
    both = ("z", "y")
    rows = z_size * short_rows

    def turn_y(value, steps):
        return lax.ppermute(value, "y", [(i, (i + steps) % y_size) for i in range(y_size)])

    def heads_of(*parts):
        stacked = jnp.stack([part.reshape(short_rows, HEADS, head_size) for part in parts], axis=2)
        return stacked.transpose(1, 0, 2, 3).reshape(HEADS, short_rows, len(parts) * head_size)

    def swap(value):
        return lax.all_to_all(value, "z", 0, 0)

    def back(value):
        parts = value.shape[2] // head_size
        split = value.reshape(HEADS, short_rows, parts, head_size).transpose(1, 2, 0, 3)
        return split.reshape(short_rows, parts, attn_width)

    d_expand = out_grad.reshape(short_rows, 4 * byte_width)
    d_expand_all = lax.all_gather(d_expand, "z", axis=0, tiled=True)
    edge = lax.ppermute(byte_input[-3:], both, [(i, i + 1) for i in range(count - 1)])
    d_attended = mm(d_expand, w_expand, NT).astype(jnp.bfloat16)
    grouped = jnp.concatenate([edge, byte_input[:-3]], axis=0).reshape(short_rows, 4 * byte_width)
    hidden = mm(grouped, w_short)
    normed, hidden_scale = unit(hidden)
    normed_b = normed.astype(jnp.bfloat16)
    projected = mm(normed_b, w_attend).astype(jnp.bfloat16)
    inputs_all = lax.all_gather(jnp.concatenate([grouped, normed_b], axis=1), "z", axis=0, tiled=True)
    query = projected[:, :attn_width]
    key = projected[:, attn_width : 2 * attn_width]
    value = projected[:, 2 * attn_width :]
    kv = swap(heads_of(key, value)).reshape(rows, 2 * head_size)
    kvs = [kv] + [turn_y(kv, step) for step in range(1, y_size)]
    qd = swap(heads_of(query, d_attended)).reshape(rows, 2 * head_size)
    y = lax.axis_index("y").astype(jnp.int32).reshape(1)
    attended, d_query, own, *sent = attention(y, qd, kvs, short_rows)

    grad_expand = lax.psum_scatter(
        mm(attended, d_expand_all, TN).astype(jnp.bfloat16), "y", scatter_dimension=0, tiled=True
    ).astype(jnp.float32)
    total = own
    for step in range(1, y_size):
        total = total + turn_y(sent[step - 1], -step).astype(jnp.float32)
    first_back = jnp.concatenate([attended, d_query], axis=1).reshape(HEADS, short_rows, 2 * head_size)
    first_back = back(swap(first_back))
    attended_own = first_back[:, 0]
    key_unit, key_scale = unit(kv[:, :head_size].astype(jnp.float32))
    d_kv = jnp.concatenate(
        [norm_back(key_unit, key_scale, total[:, :head_size]), total[:, head_size:]], axis=1
    ).astype(jnp.bfloat16)
    second_back = back(swap(d_kv.reshape(HEADS, short_rows, 2 * head_size)))
    d_projected = jnp.concatenate([first_back[:, 1], second_back[:, 0], second_back[:, 1]], axis=1)

    expanded = mm(attended_own, w_expand)
    byte_output = (
        byte_input.astype(jnp.float32) + expanded.reshape(4 * short_rows, byte_width)
    ).astype(jnp.bfloat16)

    d_normed = mm(d_projected, w_attend, NT)
    d_hidden = norm_back(normed, hidden_scale, d_normed).astype(jnp.bfloat16)
    d_hidden_cols = d_hidden.reshape(short_rows, z_size, model_width // z_size).transpose(1, 0, 2)
    d_hidden_cols = swap(d_hidden_cols).reshape(rows, model_width // z_size)
    d_grouped = mm(d_hidden, w_short, NT).astype(jnp.bfloat16).reshape(4 * short_rows, byte_width)
    back_edge = lax.ppermute(d_grouped[:3], both, [(i + 1, i) for i in range(count - 1)])
    moved = jnp.concatenate([d_grouped[3:], back_edge], axis=0).astype(jnp.float32)
    input_grad = (out_grad.astype(jnp.float32) + moved).astype(jnp.bfloat16)

    d_head = jnp.concatenate([d_query, d_kv], axis=1)
    part_attend = mm(inputs_all[:, model_width:], d_head, TN)
    part_short = mm(inputs_all[:, :model_width], d_hidden_cols, TN)
    parts = jnp.concatenate([part_attend, part_short], axis=1).astype(jnp.bfloat16)
    own_rows = model_width // count
    parts = lax.all_to_all(parts.reshape(count, own_rows, parts.shape[1]), both, 0, 0)
    parts = jnp.sum(parts.reshape(z_size, y_size, own_rows, 4, head_size).astype(jnp.float32), axis=1)
    parts = parts.transpose(1, 2, 0, 3).reshape(own_rows, 4 * attn_width)
    grad_attend = parts[:, : 3 * attn_width]
    grad_short = parts[:, 3 * attn_width :]
    return (byte_output, input_grad, grad_short, grad_attend, grad_expand)


def solution(mesh):
    docs, seq = mesh.devices.shape
    fine = Mesh(mesh.devices.reshape(docs, HEADS, seq // HEADS), ("docs", "z", "y"))
    split = P(("docs", "z", "y"), None)
    return jax.shard_map(
        local, mesh=fine, in_specs=(split, P(), P(), P(), split), out_specs=(split,) * 5, check_vma=False
    )
```

```python
import functools

import jax
import jax.numpy as jnp
from jax import lax
from jax.experimental import pallas as pl
from jax.experimental.pallas import tpu as pltpu
from jax.sharding import Mesh, PartitionSpec as P

HEADS = 8


SCORE_BOUND = 16.0
EPSILON = 1e-06

NT = (((1,), (1,)), ((), ()))
TN = (((0,), (0,)), ((), ()))


def mm(left, right, dims=(((1,), (0,)), ((), ()))):
    return lax.dot_general(left, right, dims, preferred_element_type=jnp.float32)


def unit(matrix):
    scale = lax.rsqrt(jnp.mean(matrix * matrix, axis=1, keepdims=True) + EPSILON)
    return (matrix * scale, scale)


def norm_back(normed, scale, upstream):
    inner = jnp.mean(normed * upstream, axis=1, keepdims=True)
    return scale * (upstream - normed * inner)


def chunks_of(rows, block, width=256):
    found = []
    for first in range(0, rows, width):
        found.append((first, min(width, rows - first), first // block * block))
    return found


def attention_body(block, shards, y_ref, qd_ref, *refs):
    kv_refs = refs[:shards]
    att_ref, dq_ref, own_ref = refs[shards : shards + 3]
    sent_refs = refs[shards + 3 : 2 * shards + 2]
    p_ref, kb_ref, acc_ref, dq_acc = refs[2 * shards + 2 :]
    rows, head_size = att_ref.shape
    factor = SCORE_BOUND / head_size
    chunks = chunks_of(rows, block)
    y = y_ref[0]
    query_unit, query_scale = unit(qd_ref[:, :head_size].astype(jnp.float32))
    qb = query_unit.astype(jnp.bfloat16)
    qpos = lax.broadcasted_iota(jnp.int32, (rows, 1), 0)
    start = jnp.zeros((rows, 1), jnp.int32)
    for edge in range(block, rows, block):
        start = start + jnp.where(qpos >= edge, block, 0)
    denom = jnp.zeros((rows, 1), jnp.float32)
    acc_ref[...] = jnp.zeros_like(acc_ref)
    for turn in range(shards):
        key_unit, _ = unit(kv_refs[turn][:, :head_size].astype(jnp.float32))
        kb_ref[turn] = key_unit.astype(jnp.bfloat16)
        limit = qpos + 1 if turn == 0 else start + jnp.where(y >= turn, block, 0)
        for number, (first, width, row) in enumerate(chunks):
            dots = mm(qb[row:], kb_ref[turn, first : first + width], NT)
            key_pos = first + lax.broadcasted_iota(jnp.int32, (rows - row, width), 1)
            powers = jnp.where(key_pos < limit[row:], jnp.exp(dots * factor), 0.0)
            p_ref[turn, number, row:, :width] = powers
            part = jnp.sum(powers, axis=1, keepdims=True)
            denom = denom + (part if row == 0 else jnp.concatenate([jnp.zeros((row, 1), jnp.float32), part], axis=0))
            acc_ref[row:] += mm(powers.astype(jnp.bfloat16), kv_refs[turn][first : first + width, head_size:])
    inverse = 1.0 / denom
    attended = (acc_ref[...] * inverse).astype(jnp.bfloat16)
    att_ref[...] = attended
    d_attended = qd_ref[:, head_size:].astype(jnp.float32)
    grad = (d_attended * inverse).astype(jnp.bfloat16)
    shift = jnp.sum(d_attended * attended.astype(jnp.float32), axis=1, keepdims=True) * inverse
    shift = shift.astype(jnp.bfloat16).astype(jnp.float32)
    dq_acc[...] = jnp.zeros_like(dq_acc)
    for turn in range(shards):
        out = own_ref if turn == 0 else sent_refs[turn - 1]
        for number, (first, width, row) in enumerate(chunks):
            powers = p_ref[turn, number, row:, :width]
            grad_dot = mm(grad[row:], kv_refs[turn][first : first + width, head_size:], NT)
            d_score = (powers * (grad_dot - shift[row:]) * factor).astype(jnp.bfloat16)
            dq_acc[row:] += mm(d_score, kb_ref[turn, first : first + width])
            out[first : first + width, :head_size] = mm(d_score, qb[row:], TN).astype(out.dtype)
            out[first : first + width, head_size:] = mm(powers.astype(jnp.bfloat16), grad[row:], TN).astype(out.dtype)
    dq_ref[...] = norm_back(query_unit, query_scale, dq_acc[...]).astype(jnp.bfloat16)


def attention(y, qd, kvs, block):
    rows, width = qd.shape
    head_size = width // 2
    shards = len(kvs)
    vmem = pl.BlockSpec(memory_space=pltpu.VMEM)
    shape = jax.ShapeDtypeStruct
    outs = [shape((rows, head_size), jnp.bfloat16)] * 2
    outs += [shape((rows, width), jnp.float32)] + [shape((rows, width), jnp.bfloat16)] * (shards - 1)
    return pl.pallas_call(
        functools.partial(attention_body, block, shards),
        out_shape=outs,
        in_specs=[pl.BlockSpec(memory_space=pltpu.SMEM)] + [vmem] * (shards + 1),
        out_specs=[vmem] * len(outs),
        scratch_shapes=[
            pltpu.VMEM((shards, len(chunks_of(rows, block)), rows, 256), jnp.float32),
            pltpu.VMEM((shards, rows, head_size), jnp.bfloat16),
            pltpu.VMEM((rows, head_size), jnp.float32),
            pltpu.VMEM((rows, head_size), jnp.float32),
        ],
        compiler_params=pltpu.CompilerParams(vmem_limit_bytes=40 * 1024 * 1024),
        name="attention",
    )(y, qd, *kvs)


def hidden_grad_body(y_ref, first_ref, second_ref, weight_ref, normed_ref, scale_ref, out_ref, *refs):
    cols_refs, (joined_ref,) = refs[:-1], refs[-1:]
    heads, rows, width = first_ref.shape
    lanes = width // 2
    attn_width = heads * lanes
    for head in range(heads):
        places = [part * attn_width + head * lanes for part in range(3)]
        joined_ref[:, places[0] : places[0] + lanes] = first_ref[head, :, lanes:]
        joined_ref[:, places[1] : places[1] + lanes] = second_ref[head, :, :lanes]
        joined_ref[:, places[2] : places[2] + lanes] = second_ref[head, :, lanes:]
    d_normed = mm(joined_ref[...], weight_ref[...], NT)
    out_ref[...] = norm_back(normed_ref[...], scale_ref[...], d_normed).astype(jnp.bfloat16)
    count = len(cols_refs)
    y_cols = out_ref.shape[1] // count
    for step, cols_ref in enumerate(cols_refs):
        first = pl.multiple_of(lax.rem(y_ref[0] + step, count) * y_cols, y_cols)
        cols_ref[...] = out_ref[:, pl.ds(first, y_cols)]


def hidden_grad(y, first, second, weight, normed, scale, y_size):
    rows, model_width = normed.shape
    vmem = pl.BlockSpec(memory_space=pltpu.VMEM)
    outs = [jax.ShapeDtypeStruct((rows, model_width), jnp.bfloat16)]
    outs += [jax.ShapeDtypeStruct((rows, model_width // y_size), jnp.bfloat16)] * y_size
    return pl.pallas_call(
        hidden_grad_body,
        out_shape=outs,
        in_specs=[pl.BlockSpec(memory_space=pltpu.SMEM)] + [vmem] * 5,
        out_specs=[vmem] * len(outs),
        scratch_shapes=[pltpu.VMEM((rows, weight.shape[1]), jnp.bfloat16)],
        compiler_params=pltpu.CompilerParams(vmem_limit_bytes=24 * 1024 * 1024),
        name="hidden_grad",
    )(y, first, second, weight, normed, scale)


def head_grads_body(normed_ref, dq_ref, dkv_ref, attended_ref, expand_ref, out_ref):
    shards, groups, own_rows, width = out_ref.shape
    d_head = jnp.concatenate([dq_ref[...], dkv_ref[...]], axis=1)
    attend = mm(normed_ref[...], d_head, TN).astype(out_ref.dtype)
    expand = mm(attended_ref[...], expand_ref[...], TN).astype(out_ref.dtype)
    head_width = d_head.shape[1]
    lanes = width - head_width
    for shard in range(shards):
        for group in range(groups):
            first = (group * shards + shard) * own_rows
            out_ref[shard, group, :, :head_width] = attend[first : first + own_rows]
            piece = expand[shard * own_rows : (shard + 1) * own_rows, group * lanes : (group + 1) * lanes]
            out_ref[shard, group, :, head_width:] = piece


def head_grads(normed, d_query, d_kv, attended, d_expand, groups, shards):
    model_width = normed.shape[1]
    width = 3 * d_query.shape[1] + d_expand.shape[1] // groups
    vmem = pl.BlockSpec(memory_space=pltpu.VMEM)
    return pl.pallas_call(
        head_grads_body,
        out_shape=jax.ShapeDtypeStruct((shards, groups, model_width // groups // shards, width), jnp.bfloat16),
        in_specs=[vmem] * 5,
        out_specs=vmem,
        compiler_params=pltpu.CompilerParams(vmem_limit_bytes=24 * 1024 * 1024),
        name="head_grads",
    )(normed, d_query, d_kv, attended, d_expand)


def split_parts_body(z_ref, parts_ref, expand_ref, *piece_refs):
    groups, _, width = parts_ref.shape
    head_width = piece_refs[0].shape[1]
    lanes = width - head_width
    for group in range(groups):
        expand_ref[:, group * lanes : (group + 1) * lanes] = parts_ref[group, :, head_width:].astype(jnp.float32)
    for step, piece_ref in enumerate(piece_refs):
        piece_ref[...] = parts_ref[lax.rem(z_ref[0] + step, groups), :, :head_width]


def split_parts(z, parts, head_width):
    groups, own_rows, width = parts.shape
    vmem = pl.BlockSpec(memory_space=pltpu.VMEM)
    outs = [jax.ShapeDtypeStruct((own_rows, (width - head_width) * groups), jnp.float32)]
    outs += [jax.ShapeDtypeStruct((own_rows, head_width), jnp.bfloat16)] * groups
    return pl.pallas_call(
        split_parts_body,
        out_shape=outs,
        in_specs=[pl.BlockSpec(memory_space=pltpu.SMEM), vmem],
        out_specs=[vmem] * len(outs),
        name="split_parts",
    )(z, parts)


def short_grads_body(shards, *refs):
    grouped_refs, cols_refs, out_ref = refs[:shards], refs[shards : 2 * shards], refs[-1]
    count, tall, lanes = out_ref.shape
    grouped = jnp.concatenate([ref[...] for ref in grouped_refs], axis=0)
    cols = jnp.concatenate([ref[...] for ref in cols_refs], axis=0)
    short = mm(grouped, cols, TN).astype(jnp.bfloat16)
    parts = short.shape[1] // lanes
    own_rows = tall // parts
    for part in range(parts):
        piece = short[:, part * lanes : (part + 1) * lanes].reshape(count, own_rows, lanes)
        out_ref[:, part * own_rows : (part + 1) * own_rows, :] = piece


def short_grads(grouped, cols, count, lanes):
    tall = grouped[0].shape[1] // count * (cols[0].shape[1] // lanes)
    vmem = pl.BlockSpec(memory_space=pltpu.VMEM)
    return pl.pallas_call(
        functools.partial(short_grads_body, len(grouped)),
        out_shape=jax.ShapeDtypeStruct((count, tall, lanes), jnp.bfloat16),
        in_specs=[vmem] * (2 * len(grouped)),
        out_specs=vmem,
        name="short_grads",
    )(*grouped, *cols)


def assemble_attend_body(z_ref, *refs):
    piece_refs, out_ref = refs[:-1], refs[-1]
    groups = len(piece_refs)
    lanes = piece_refs[0].shape[1] // 3
    for step, piece_ref in enumerate(piece_refs):
        head = lax.rem(z_ref[0] + (groups - step), groups)
        for part in range(3):
            first = pl.multiple_of((part * groups + head) * lanes, lanes)
            piece = piece_ref[:, part * lanes : (part + 1) * lanes].astype(jnp.float32)
            out_ref[:, pl.ds(first, lanes)] = piece


def assemble_attend(z, pieces):
    own_rows, width = pieces[0].shape
    vmem = pl.BlockSpec(memory_space=pltpu.VMEM)
    return pl.pallas_call(
        assemble_attend_body,
        out_shape=jax.ShapeDtypeStruct((own_rows, width * len(pieces)), jnp.float32),
        in_specs=[pl.BlockSpec(memory_space=pltpu.SMEM)] + [vmem] * len(pieces),
        out_specs=vmem,
        name="assemble_attend",
    )(z, *pieces)


def assemble_short_body(shards, parts_ref, out_ref):
    count, tall, lanes = parts_ref.shape
    own_rows, model_width = out_ref.shape
    parts = tall // own_rows
    for shard in range(shards):
        total = jnp.zeros((tall, lanes), jnp.float32)
        for group in range(count // shards):
            total = total + parts_ref[group * shards + shard].astype(jnp.float32)
        for part in range(parts):
            first = (shard * parts + part) * lanes
            out_ref[:, first : first + lanes] = total[part * own_rows : (part + 1) * own_rows]


def assemble_short(parts, own_rows, model_width, shards):
    vmem = pl.BlockSpec(memory_space=pltpu.VMEM)
    return pl.pallas_call(
        functools.partial(assemble_short_body, shards),
        out_shape=jax.ShapeDtypeStruct((own_rows, model_width), jnp.float32),
        in_specs=[vmem],
        out_specs=vmem,
        name="assemble_short",
    )(parts)


def tie(*values):
    return lax.optimization_barrier(values)


def local(byte_input, w_short, w_attend, w_expand, out_grad):
    z_size, y_size = lax.axis_size("z"), lax.axis_size("y")
    count = z_size * y_size
    short_rows = byte_input.shape[0] // 4
    byte_width = byte_input.shape[1]
    attn_width = w_attend.shape[1] // 3
    model_width = w_short.shape[1]
    head_size = attn_width // HEADS
    both = ("z", "y")
    rows = z_size * short_rows

    def turn_y(value, steps):
        return lax.ppermute(value, "y", [(i, (i + steps) % y_size) for i in range(y_size)])

    def heads_of(*parts):
        stacked = jnp.stack([part.reshape(short_rows, HEADS, head_size) for part in parts], axis=2)
        return stacked.transpose(1, 0, 2, 3).reshape(HEADS, short_rows, len(parts) * head_size)

    def swap(value):
        return lax.all_to_all(value, "z", 0, 0)

    d_expand = out_grad.reshape(short_rows, 4 * byte_width)
    edge = lax.ppermute(byte_input[-3:], both, [(i, i + 1) for i in range(count - 1)])
    d_attended = mm(d_expand, w_expand, NT).astype(jnp.bfloat16)
    grouped = jnp.concatenate([edge, byte_input[:-3]], axis=0).reshape(short_rows, 4 * byte_width)
    hidden = mm(grouped, w_short)
    normed, hidden_scale = unit(hidden)
    normed_b = normed.astype(jnp.bfloat16)
    projected = mm(normed_b, w_attend).astype(jnp.bfloat16)
    key = projected[:, attn_width : 2 * attn_width]
    value = projected[:, 2 * attn_width :]
    kv = swap(heads_of(key, value)).reshape(rows, 2 * head_size)
    qd = heads_of(projected[:, :attn_width], d_attended)
    grouped_y = [grouped] + [turn_y(grouped, step) for step in range(1, y_size)]
    kv, qd, gathered, *grouped_y = tie(kv, qd, jnp.concatenate([d_expand, normed_b], axis=1), *grouped_y)
    gathered = lax.all_gather(gathered, "z", axis=0, tiled=True)
    d_expand_all, normed_all = gathered[:, : 4 * byte_width], gathered[:, 4 * byte_width :]
    kvs = [kv] + [turn_y(kv, step) for step in range(1, y_size)]
    qd = swap(qd).reshape(rows, 2 * head_size)
    y = lax.axis_index("y").astype(jnp.int32).reshape(1)
    attended, d_query, own, *sent = attention(y, qd, kvs, short_rows)

    own_rows = model_width // count
    arrived = [turn_y(sent[step - 1], -step) for step in range(1, y_size)]
    total = own
    for part in arrived:
        total = total + part.astype(jnp.float32)
    first_back = jnp.concatenate([attended, d_query], axis=1).reshape(HEADS, short_rows, 2 * head_size)
    first_back = swap(first_back)
    key_unit, key_scale = unit(kv[:, :head_size].astype(jnp.float32))
    d_kv = jnp.concatenate(
        [norm_back(key_unit, key_scale, total[:, :head_size]), total[:, head_size:]], axis=1
    ).astype(jnp.bfloat16)
    first_back, d_kv = tie(first_back, d_kv)
    second_back = swap(d_kv.reshape(HEADS, short_rows, 2 * head_size))
    parts = head_grads(normed_all, d_query, d_kv, attended, d_expand_all, z_size, y_size)
    second_back, parts = tie(second_back, parts)
    parts = lax.psum_scatter(parts, "y", scatter_dimension=0)
    d_hidden, *d_hidden_y = hidden_grad(y, first_back, second_back, w_attend, normed, hidden_scale, y_size)
    d_hidden_y = d_hidden_y[:1] + [turn_y(d_hidden_y[step], step) for step in range(1, y_size)]
    d_grouped = mm(d_hidden, w_short, NT).astype(jnp.bfloat16).reshape(4 * short_rows, byte_width)
    *d_hidden_y, d_grouped = tie(*d_hidden_y, d_grouped)
    short = short_grads(grouped_y, d_hidden_y, count, head_size)
    short, first_back = tie(short, first_back)
    short = lax.all_to_all(short, both, 0, 0)
    z = lax.axis_index("z").astype(jnp.int32).reshape(1)
    grad_expand, *pieces = split_parts(z, parts, 3 * head_size)
    pieces = pieces[:1] + [
        lax.ppermute(pieces[step], "z", [(i, (i + step) % z_size) for i in range(z_size)])
        for step in range(1, z_size)
    ]
    grad_attend = assemble_attend(z, pieces)
    attended_own = first_back[:, :, :head_size].transpose(1, 0, 2).reshape(short_rows, attn_width)
    expanded = mm(attended_own, w_expand)
    byte_output = (
        byte_input.astype(jnp.float32) + expanded.reshape(4 * short_rows, byte_width)
    ).astype(jnp.bfloat16)
    back_edge = lax.ppermute(d_grouped[:3], both, [(i + 1, i) for i in range(count - 1)])
    moved = jnp.concatenate([d_grouped[3:], back_edge], axis=0).astype(jnp.float32)
    input_grad = (out_grad.astype(jnp.float32) + moved).astype(jnp.bfloat16)
    short, input_grad, byte_output, grad_attend = tie(short, input_grad, byte_output, grad_attend)
    grad_short = assemble_short(short, own_rows, model_width, y_size)
    return (byte_output, input_grad, grad_short, grad_attend, grad_expand)


def solution(mesh):
    docs, seq = mesh.devices.shape
    fine = Mesh(mesh.devices.reshape(docs, HEADS, seq // HEADS), ("docs", "z", "y"))
    split = P(("docs", "z", "y"), None)
    return jax.shard_map(
        local, mesh=fine, in_specs=(split, P(), P(), P(), split), out_specs=(split,) * 5, check_vma=False
    )
```

```python
import functools

import jax
import jax.numpy as jnp
from jax import lax
from jax.experimental import pallas as pl
from jax.experimental.pallas import tpu as pltpu
from jax.sharding import Mesh, PartitionSpec as P

HEADS = 8


SCORE_BOUND = 16.0
EPSILON = 1e-06

NT = (((1,), (1,)), ((), ()))
TN = (((0,), (0,)), ((), ()))


def mm(left, right, dims=(((1,), (0,)), ((), ()))):
    return lax.dot_general(left, right, dims, preferred_element_type=jnp.float32)


def unit(matrix):
    scale = lax.rsqrt(jnp.mean(matrix * matrix, axis=1, keepdims=True) + EPSILON)
    return (matrix * scale, scale)


def norm_back(normed, scale, upstream):
    inner = jnp.mean(normed * upstream, axis=1, keepdims=True)
    return scale * (upstream - normed * inner)


def chunks_of(rows, block, width=256):
    found = []
    for first in range(0, rows, width):
        found.append((first, min(width, rows - first), first // block * block))
    return found


def attention_body(block, shards, y_ref, qd_ref, *refs):
    kv_refs = refs[:shards]
    att_ref, dq_ref, own_ref = refs[shards : shards + 3]
    sent_refs = refs[shards + 3 : 2 * shards + 2]
    p_ref, kb_ref, acc_ref, dq_acc = refs[2 * shards + 2 :]
    rows, head_size = att_ref.shape
    factor = SCORE_BOUND / head_size
    chunks = chunks_of(rows, block)
    y = y_ref[0]
    query_unit, query_scale = unit(qd_ref[:, :head_size].astype(jnp.float32))
    qb = query_unit.astype(jnp.bfloat16)
    qpos = lax.broadcasted_iota(jnp.int32, (rows, 1), 0)
    start = jnp.zeros((rows, 1), jnp.int32)
    for edge in range(block, rows, block):
        start = start + jnp.where(qpos >= edge, block, 0)
    denom = jnp.zeros((rows, 1), jnp.float32)
    acc_ref[...] = jnp.zeros_like(acc_ref)
    for turn in range(shards):
        key_unit, _ = unit(kv_refs[turn][:, :head_size].astype(jnp.float32))
        kb_ref[turn] = key_unit.astype(jnp.bfloat16)
        limit = qpos + 1 if turn == 0 else start + jnp.where(y >= turn, block, 0)
        for number, (first, width, row) in enumerate(chunks):
            dots = mm(qb[row:], kb_ref[turn, first : first + width], NT)
            key_pos = first + lax.broadcasted_iota(jnp.int32, (rows - row, width), 1)
            powers = jnp.where(key_pos < limit[row:], jnp.exp(dots * factor), 0.0)
            p_ref[turn, number, row:, :width] = powers
            part = jnp.sum(powers, axis=1, keepdims=True)
            denom = denom + (part if row == 0 else jnp.concatenate([jnp.zeros((row, 1), jnp.float32), part], axis=0))
            acc_ref[row:] += mm(powers.astype(jnp.bfloat16), kv_refs[turn][first : first + width, head_size:])
    inverse = 1.0 / denom
    attended = (acc_ref[...] * inverse).astype(jnp.bfloat16)
    att_ref[...] = attended
    d_attended = qd_ref[:, head_size:].astype(jnp.float32)
    grad = (d_attended * inverse).astype(jnp.bfloat16)
    shift = jnp.sum(d_attended * attended.astype(jnp.float32), axis=1, keepdims=True) * inverse
    shift = shift.astype(jnp.bfloat16).astype(jnp.float32)
    dq_acc[...] = jnp.zeros_like(dq_acc)
    for turn in range(shards):
        out = own_ref if turn == 0 else sent_refs[turn - 1]
        for number, (first, width, row) in enumerate(chunks):
            powers = p_ref[turn, number, row:, :width]
            grad_dot = mm(grad[row:], kv_refs[turn][first : first + width, head_size:], NT)
            d_score = (powers * (grad_dot - shift[row:]) * factor).astype(jnp.bfloat16)
            dq_acc[row:] += mm(d_score, kb_ref[turn, first : first + width])
            out[first : first + width, :head_size] = mm(d_score, qb[row:], TN).astype(out.dtype)
            out[first : first + width, head_size:] = mm(powers.astype(jnp.bfloat16), grad[row:], TN).astype(out.dtype)
    dq_ref[...] = norm_back(query_unit, query_scale, dq_acc[...]).astype(jnp.bfloat16)


def attention(y, qd, kvs, block):
    rows, width = qd.shape
    head_size = width // 2
    shards = len(kvs)
    vmem = pl.BlockSpec(memory_space=pltpu.VMEM)
    shape = jax.ShapeDtypeStruct
    outs = [shape((rows, head_size), jnp.bfloat16)] * 2
    outs += [shape((rows, width), jnp.float32)] + [shape((rows, width), jnp.bfloat16)] * (shards - 1)
    return pl.pallas_call(
        functools.partial(attention_body, block, shards),
        out_shape=outs,
        in_specs=[pl.BlockSpec(memory_space=pltpu.SMEM)] + [vmem] * (shards + 1),
        out_specs=[vmem] * len(outs),
        scratch_shapes=[
            pltpu.VMEM((shards, len(chunks_of(rows, block)), rows, 256), jnp.float32),
            pltpu.VMEM((shards, rows, head_size), jnp.bfloat16),
            pltpu.VMEM((rows, head_size), jnp.float32),
            pltpu.VMEM((rows, head_size), jnp.float32),
        ],
        compiler_params=pltpu.CompilerParams(vmem_limit_bytes=40 * 1024 * 1024),
        name="attention",
    )(y, qd, *kvs)


def hidden_grad_body(y_ref, first_ref, second_ref, weight_ref, normed_ref, scale_ref, out_ref, *refs):
    cols_refs, (joined_ref,) = refs[:-1], refs[-1:]
    heads, rows, width = first_ref.shape
    lanes = width // 2
    attn_width = heads * lanes
    for head in range(heads):
        places = [part * attn_width + head * lanes for part in range(3)]
        joined_ref[:, places[0] : places[0] + lanes] = first_ref[head, :, lanes:]
        joined_ref[:, places[1] : places[1] + lanes] = second_ref[head, :, :lanes]
        joined_ref[:, places[2] : places[2] + lanes] = second_ref[head, :, lanes:]
    d_normed = mm(joined_ref[...], weight_ref[...], NT)
    out_ref[...] = norm_back(normed_ref[...], scale_ref[...], d_normed).astype(jnp.bfloat16)
    count = len(cols_refs)
    y_cols = out_ref.shape[1] // count
    for step, cols_ref in enumerate(cols_refs):
        first = pl.multiple_of(lax.rem(y_ref[0] + step, count) * y_cols, y_cols)
        cols_ref[...] = out_ref[:, pl.ds(first, y_cols)]


def hidden_grad(y, first, second, weight, normed, scale, y_size):
    rows, model_width = normed.shape
    vmem = pl.BlockSpec(memory_space=pltpu.VMEM)
    outs = [jax.ShapeDtypeStruct((rows, model_width), jnp.bfloat16)]
    outs += [jax.ShapeDtypeStruct((rows, model_width // y_size), jnp.bfloat16)] * y_size
    return pl.pallas_call(
        hidden_grad_body,
        out_shape=outs,
        in_specs=[pl.BlockSpec(memory_space=pltpu.SMEM)] + [vmem] * 5,
        out_specs=[vmem] * len(outs),
        scratch_shapes=[pltpu.VMEM((rows, weight.shape[1]), jnp.bfloat16)],
        compiler_params=pltpu.CompilerParams(vmem_limit_bytes=24 * 1024 * 1024),
        name="hidden_grad",
    )(y, first, second, weight, normed, scale)


def head_grads_body(gathered_ref, dq_ref, dkv_ref, attended_ref, out_ref):
    shards, groups, own_rows, width = out_ref.shape
    model_width = groups * shards * own_rows
    d_head = jnp.concatenate([dq_ref[...], dkv_ref[...]], axis=1)
    attend = mm(gathered_ref[:, gathered_ref.shape[1] - model_width :], d_head, TN).astype(out_ref.dtype)
    expand = mm(attended_ref[...], gathered_ref[:, : gathered_ref.shape[1] - model_width], TN).astype(out_ref.dtype)
    head_width = d_head.shape[1]
    lanes = width - head_width
    for shard in range(shards):
        for group in range(groups):
            first = (group * shards + shard) * own_rows
            out_ref[shard, group, :, :head_width] = attend[first : first + own_rows]
            piece = expand[shard * own_rows : (shard + 1) * own_rows, group * lanes : (group + 1) * lanes]
            out_ref[shard, group, :, head_width:] = piece


def head_grads(gathered, d_query, d_kv, attended, model_width, groups, shards):
    width = 3 * d_query.shape[1] + (gathered.shape[1] - model_width) // groups
    vmem = pl.BlockSpec(memory_space=pltpu.VMEM)
    return pl.pallas_call(
        head_grads_body,
        out_shape=jax.ShapeDtypeStruct((shards, groups, model_width // groups // shards, width), jnp.bfloat16),
        in_specs=[vmem] * 4,
        out_specs=vmem,
        compiler_params=pltpu.CompilerParams(vmem_limit_bytes=24 * 1024 * 1024),
        name="head_grads",
    )(gathered, d_query, d_kv, attended)


def split_parts_body(z_ref, parts_ref, expand_ref, *piece_refs):
    groups, _, width = parts_ref.shape
    head_width = piece_refs[0].shape[1]
    lanes = width - head_width
    for group in range(groups):
        expand_ref[:, group * lanes : (group + 1) * lanes] = parts_ref[group, :, head_width:].astype(jnp.float32)
    for step, piece_ref in enumerate(piece_refs):
        piece_ref[...] = parts_ref[lax.rem(z_ref[0] + step, groups), :, :head_width]


def split_parts(z, parts, head_width):
    groups, own_rows, width = parts.shape
    vmem = pl.BlockSpec(memory_space=pltpu.VMEM)
    outs = [jax.ShapeDtypeStruct((own_rows, (width - head_width) * groups), jnp.float32)]
    outs += [jax.ShapeDtypeStruct((own_rows, head_width), jnp.bfloat16)] * groups
    return pl.pallas_call(
        split_parts_body,
        out_shape=outs,
        in_specs=[pl.BlockSpec(memory_space=pltpu.SMEM), vmem],
        out_specs=[vmem] * len(outs),
        name="split_parts",
    )(z, parts)


def short_grads_body(shards, *refs):
    grouped_refs, cols_refs, out_ref = refs[:shards], refs[shards : 2 * shards], refs[-1]
    count, tall, lanes = out_ref.shape
    grouped = jnp.concatenate([ref[...] for ref in grouped_refs], axis=0)
    cols = jnp.concatenate([ref[...] for ref in cols_refs], axis=0)
    short = mm(grouped, cols, TN).astype(jnp.bfloat16)
    parts = short.shape[1] // lanes
    own_rows = tall // parts
    for part in range(parts):
        piece = short[:, part * lanes : (part + 1) * lanes].reshape(count, own_rows, lanes)
        out_ref[:, part * own_rows : (part + 1) * own_rows, :] = piece


def short_grads(grouped, cols, count, lanes):
    tall = grouped[0].shape[1] // count * (cols[0].shape[1] // lanes)
    vmem = pl.BlockSpec(memory_space=pltpu.VMEM)
    return pl.pallas_call(
        functools.partial(short_grads_body, len(grouped)),
        out_shape=jax.ShapeDtypeStruct((count, tall, lanes), jnp.bfloat16),
        in_specs=[vmem] * (2 * len(grouped)),
        out_specs=vmem,
        name="short_grads",
    )(*grouped, *cols)


def assemble_attend_body(z_ref, *refs):
    piece_refs, out_ref = refs[:-1], refs[-1]
    groups = len(piece_refs)
    lanes = piece_refs[0].shape[1] // 3
    for step, piece_ref in enumerate(piece_refs):
        head = lax.rem(z_ref[0] + (groups - step), groups)
        for part in range(3):
            first = pl.multiple_of((part * groups + head) * lanes, lanes)
            piece = piece_ref[:, part * lanes : (part + 1) * lanes].astype(jnp.float32)
            out_ref[:, pl.ds(first, lanes)] = piece


def assemble_attend(z, pieces):
    own_rows, width = pieces[0].shape
    vmem = pl.BlockSpec(memory_space=pltpu.VMEM)
    return pl.pallas_call(
        assemble_attend_body,
        out_shape=jax.ShapeDtypeStruct((own_rows, width * len(pieces)), jnp.float32),
        in_specs=[pl.BlockSpec(memory_space=pltpu.SMEM)] + [vmem] * len(pieces),
        out_specs=vmem,
        name="assemble_attend",
    )(z, *pieces)


def assemble_short_body(shards, parts_ref, out_ref):
    count, tall, lanes = parts_ref.shape
    own_rows, model_width = out_ref.shape
    parts = tall // own_rows
    for shard in range(shards):
        total = jnp.zeros((tall, lanes), jnp.float32)
        for group in range(count // shards):
            total = total + parts_ref[group * shards + shard].astype(jnp.float32)
        for part in range(parts):
            first = (shard * parts + part) * lanes
            out_ref[:, first : first + lanes] = total[part * own_rows : (part + 1) * own_rows]


def assemble_short(parts, own_rows, model_width, shards):
    vmem = pl.BlockSpec(memory_space=pltpu.VMEM)
    return pl.pallas_call(
        functools.partial(assemble_short_body, shards),
        out_shape=jax.ShapeDtypeStruct((own_rows, model_width), jnp.float32),
        in_specs=[vmem],
        out_specs=vmem,
        name="assemble_short",
    )(parts)


def tie(*values):
    return lax.optimization_barrier(values)


def local(byte_input, w_short, w_attend, w_expand, out_grad):
    z_size, y_size = lax.axis_size("z"), lax.axis_size("y")
    count = z_size * y_size
    short_rows = byte_input.shape[0] // 4
    byte_width = byte_input.shape[1]
    attn_width = w_attend.shape[1] // 3
    model_width = w_short.shape[1]
    head_size = attn_width // HEADS
    both = ("z", "y")
    rows = z_size * short_rows

    def turn_y(value, steps):
        return lax.ppermute(value, "y", [(i, (i + steps) % y_size) for i in range(y_size)])

    def heads_of(*parts):
        stacked = jnp.stack([part.reshape(short_rows, HEADS, head_size) for part in parts], axis=2)
        return stacked.transpose(1, 0, 2, 3).reshape(HEADS, short_rows, len(parts) * head_size)

    def swap(value):
        return lax.all_to_all(value, "z", 0, 0)

    d_expand = out_grad.reshape(short_rows, 4 * byte_width)
    edge = lax.ppermute(byte_input[-3:], both, [(i, i + 1) for i in range(count - 1)])
    d_attended = mm(d_expand, w_expand, NT).astype(jnp.bfloat16)
    grouped = jnp.concatenate([edge, byte_input[:-3]], axis=0).reshape(short_rows, 4 * byte_width)
    hidden = mm(grouped, w_short)
    normed, hidden_scale = unit(hidden)
    normed_b = normed.astype(jnp.bfloat16)
    projected = mm(normed_b, w_attend).astype(jnp.bfloat16)
    key = projected[:, attn_width : 2 * attn_width]
    value = projected[:, 2 * attn_width :]
    kv = swap(heads_of(key, value)).reshape(rows, 2 * head_size)
    qd = heads_of(projected[:, :attn_width], d_attended)
    grouped_y = [grouped] + [turn_y(grouped, step) for step in range(1, y_size)]
    kv, qd, gathered, *grouped_y = tie(kv, qd, jnp.concatenate([d_expand, normed_b], axis=1), *grouped_y)
    gathered = lax.all_gather(gathered, "z", axis=0, tiled=True)
    kvs = [kv] + [turn_y(kv, step) for step in range(1, y_size)]
    qd = swap(qd).reshape(rows, 2 * head_size)
    y = lax.axis_index("y").astype(jnp.int32).reshape(1)
    attended, d_query, own, *sent = attention(y, qd, kvs, short_rows)

    own_rows = model_width // count
    arrived = [turn_y(sent[step - 1], -step) for step in range(1, y_size)]
    total = own
    for part in arrived:
        total = total + part.astype(jnp.float32)
    first_back = jnp.concatenate([attended, d_query], axis=1).reshape(HEADS, short_rows, 2 * head_size)
    first_back = swap(first_back)
    key_unit, key_scale = unit(kv[:, :head_size].astype(jnp.float32))
    d_kv = jnp.concatenate(
        [norm_back(key_unit, key_scale, total[:, :head_size]), total[:, head_size:]], axis=1
    ).astype(jnp.bfloat16)
    first_back, d_kv = tie(first_back, d_kv)
    parts = head_grads(gathered, d_query, d_kv, attended, model_width, z_size, y_size)
    parts, d_kv = tie(parts, d_kv)
    second_back = swap(d_kv.reshape(HEADS, short_rows, 2 * head_size))
    parts = lax.psum_scatter(parts, "y", scatter_dimension=0)
    d_hidden, *d_hidden_y = hidden_grad(y, first_back, second_back, w_attend, normed, hidden_scale, y_size)
    d_hidden_y = d_hidden_y[:1] + [turn_y(d_hidden_y[step], step) for step in range(1, y_size)]
    d_grouped = mm(d_hidden, w_short, NT).astype(jnp.bfloat16).reshape(4 * short_rows, byte_width)
    *d_hidden_y, d_grouped = tie(*d_hidden_y, d_grouped)
    short = short_grads(grouped_y, d_hidden_y, count, head_size)
    short, first_back = tie(short, first_back)
    short = lax.all_to_all(short, both, 0, 0)
    z = lax.axis_index("z").astype(jnp.int32).reshape(1)
    grad_expand, *pieces = split_parts(z, parts, 3 * head_size)
    pieces = pieces[:1] + [
        lax.ppermute(pieces[step], "z", [(i, (i + step) % z_size) for i in range(z_size)])
        for step in range(1, z_size)
    ]
    grad_attend = assemble_attend(z, pieces)
    attended_own = first_back[:, :, :head_size].transpose(1, 0, 2).reshape(short_rows, attn_width)
    expanded = mm(attended_own, w_expand)
    byte_output = (
        byte_input.astype(jnp.float32) + expanded.reshape(4 * short_rows, byte_width)
    ).astype(jnp.bfloat16)
    back_edge = lax.ppermute(d_grouped[:3], both, [(i + 1, i) for i in range(count - 1)])
    moved = jnp.concatenate([d_grouped[3:], back_edge], axis=0).astype(jnp.float32)
    input_grad = (out_grad.astype(jnp.float32) + moved).astype(jnp.bfloat16)
    short, input_grad, byte_output, grad_attend = tie(short, input_grad, byte_output, grad_attend)
    grad_short = assemble_short(short, own_rows, model_width, y_size)
    return (byte_output, input_grad, grad_short, grad_attend, grad_expand)


def solution(mesh):
    docs, seq = mesh.devices.shape
    fine = Mesh(mesh.devices.reshape(docs, HEADS, seq // HEADS), ("docs", "z", "y"))
    split = P(("docs", "z", "y"), None)
    return jax.shard_map(
        local, mesh=fine, in_specs=(split, P(), P(), P(), split), out_specs=(split,) * 5, check_vma=False
    )
```

```python
import functools

import jax
import jax.numpy as jnp
from jax import lax
from jax.experimental import pallas as pl
from jax.experimental.pallas import tpu as pltpu
from jax.sharding import Mesh, PartitionSpec as P

HEADS = 8


SCORE_BOUND = 16.0
EPSILON = 1e-06

NT = (((1,), (1,)), ((), ()))
TN = (((0,), (0,)), ((), ()))


def mm(left, right, dims=(((1,), (0,)), ((), ()))):
    return lax.dot_general(left, right, dims, preferred_element_type=jnp.float32)


def unit(matrix):
    scale = lax.rsqrt(jnp.mean(matrix * matrix, axis=1, keepdims=True) + EPSILON)
    return (matrix * scale, scale)


def norm_back(normed, scale, upstream):
    inner = jnp.mean(normed * upstream, axis=1, keepdims=True)
    return scale * (upstream - normed * inner)


def chunks_of(rows, block, width=256):
    found = []
    for first in range(0, rows, width):
        found.append((first, min(width, rows - first), first // block * block))
    return found


def attention_body(block, shards, y_ref, qd_ref, *refs):
    kv_refs = refs[:shards]
    att_ref, dq_ref, own_ref = refs[shards : shards + 3]
    sent_refs = refs[shards + 3 : 2 * shards + 2]
    p_ref, kb_ref, acc_ref, dq_acc = refs[2 * shards + 2 :]
    rows, head_size = att_ref.shape
    factor = SCORE_BOUND / head_size
    chunks = chunks_of(rows, block)
    y = y_ref[0]
    query_unit, query_scale = unit(qd_ref[:, :head_size].astype(jnp.float32))
    qb = query_unit.astype(jnp.bfloat16)
    qpos = lax.broadcasted_iota(jnp.int32, (rows, 1), 0)
    start = jnp.zeros((rows, 1), jnp.int32)
    for edge in range(block, rows, block):
        start = start + jnp.where(qpos >= edge, block, 0)
    denom = jnp.zeros((rows, 1), jnp.float32)
    acc_ref[...] = jnp.zeros_like(acc_ref)
    for turn in range(shards):
        key_unit, _ = unit(kv_refs[turn][:, :head_size].astype(jnp.float32))
        kb_ref[turn] = key_unit.astype(jnp.bfloat16)
        limit = qpos + 1 if turn == 0 else start + jnp.where(y >= turn, block, 0)
        for number, (first, width, row) in enumerate(chunks):
            dots = mm(qb[row:], kb_ref[turn, first : first + width], NT)
            key_pos = first + lax.broadcasted_iota(jnp.int32, (rows - row, width), 1)
            powers = jnp.where(key_pos < limit[row:], jnp.exp(dots * factor), 0.0)
            p_ref[turn, number, row:, :width] = powers
            part = jnp.sum(powers, axis=1, keepdims=True)
            denom = denom + (part if row == 0 else jnp.concatenate([jnp.zeros((row, 1), jnp.float32), part], axis=0))
            acc_ref[row:] += mm(powers.astype(jnp.bfloat16), kv_refs[turn][first : first + width, head_size:])
    inverse = 1.0 / denom
    attended = (acc_ref[...] * inverse).astype(jnp.bfloat16)
    att_ref[...] = attended
    d_attended = qd_ref[:, head_size:].astype(jnp.float32)
    grad = (d_attended * inverse).astype(jnp.bfloat16)
    shift = jnp.sum(d_attended * attended.astype(jnp.float32), axis=1, keepdims=True) * inverse
    shift = shift.astype(jnp.bfloat16).astype(jnp.float32)
    dq_acc[...] = jnp.zeros_like(dq_acc)
    for turn in range(shards):
        out = own_ref if turn == 0 else sent_refs[turn - 1]
        for number, (first, width, row) in enumerate(chunks):
            powers = p_ref[turn, number, row:, :width]
            grad_dot = mm(grad[row:], kv_refs[turn][first : first + width, head_size:], NT)
            d_score = (powers * (grad_dot - shift[row:]) * factor).astype(jnp.bfloat16)
            dq_acc[row:] += mm(d_score, kb_ref[turn, first : first + width])
            out[first : first + width, :head_size] = mm(d_score, qb[row:], TN).astype(out.dtype)
            out[first : first + width, head_size:] = mm(powers.astype(jnp.bfloat16), grad[row:], TN).astype(out.dtype)
    dq_ref[...] = norm_back(query_unit, query_scale, dq_acc[...]).astype(jnp.bfloat16)


def attention(y, qd, kvs, block):
    rows, width = qd.shape
    head_size = width // 2
    shards = len(kvs)
    vmem = pl.BlockSpec(memory_space=pltpu.VMEM)
    shape = jax.ShapeDtypeStruct
    outs = [shape((rows, head_size), jnp.bfloat16)] * 2
    outs += [shape((rows, width), jnp.float32)] + [shape((rows, width), jnp.bfloat16)] * (shards - 1)
    return pl.pallas_call(
        functools.partial(attention_body, block, shards),
        out_shape=outs,
        in_specs=[pl.BlockSpec(memory_space=pltpu.SMEM)] + [vmem] * (shards + 1),
        out_specs=[vmem] * len(outs),
        scratch_shapes=[
            pltpu.VMEM((shards, len(chunks_of(rows, block)), rows, 256), jnp.float32),
            pltpu.VMEM((shards, rows, head_size), jnp.bfloat16),
            pltpu.VMEM((rows, head_size), jnp.float32),
            pltpu.VMEM((rows, head_size), jnp.float32),
        ],
        compiler_params=pltpu.CompilerParams(vmem_limit_bytes=40 * 1024 * 1024),
        name="attention",
    )(y, qd, *kvs)


def hidden_grad_body(y_ref, first_ref, second_ref, weight_ref, normed_ref, scale_ref, out_ref, *refs):
    cols_refs, (joined_ref,) = refs[:-1], refs[-1:]
    heads, rows, width = first_ref.shape
    lanes = width // 2
    attn_width = heads * lanes
    for head in range(heads):
        places = [part * attn_width + head * lanes for part in range(3)]
        joined_ref[:, places[0] : places[0] + lanes] = first_ref[head, :, lanes:]
        joined_ref[:, places[1] : places[1] + lanes] = second_ref[head, :, :lanes]
        joined_ref[:, places[2] : places[2] + lanes] = second_ref[head, :, lanes:]
    d_normed = mm(joined_ref[...], weight_ref[...], NT)
    out_ref[...] = norm_back(normed_ref[...], scale_ref[...], d_normed).astype(jnp.bfloat16)
    count = len(cols_refs)
    y_cols = out_ref.shape[1] // count
    for step, cols_ref in enumerate(cols_refs):
        first = pl.multiple_of(lax.rem(y_ref[0] + step, count) * y_cols, y_cols)
        cols_ref[...] = out_ref[:, pl.ds(first, y_cols)]


def hidden_grad(y, first, second, weight, normed, scale, y_size):
    rows, model_width = normed.shape
    vmem = pl.BlockSpec(memory_space=pltpu.VMEM)
    outs = [jax.ShapeDtypeStruct((rows, model_width), jnp.bfloat16)]
    outs += [jax.ShapeDtypeStruct((rows, model_width // y_size), jnp.bfloat16)] * y_size
    return pl.pallas_call(
        hidden_grad_body,
        out_shape=outs,
        in_specs=[pl.BlockSpec(memory_space=pltpu.SMEM)] + [vmem] * 5,
        out_specs=[vmem] * len(outs),
        scratch_shapes=[pltpu.VMEM((rows, weight.shape[1]), jnp.bfloat16)],
        compiler_params=pltpu.CompilerParams(vmem_limit_bytes=24 * 1024 * 1024),
        name="hidden_grad",
    )(y, first, second, weight, normed, scale)


def head_grads_body(gathered_ref, dq_ref, dkv_ref, attended_ref, out_ref):
    shards, groups, own_rows, width = out_ref.shape
    model_width = groups * shards * own_rows
    d_head = jnp.concatenate([dq_ref[...], dkv_ref[...]], axis=1)
    attend = mm(gathered_ref[:, gathered_ref.shape[1] - model_width :], d_head, TN).astype(out_ref.dtype)
    expand = mm(attended_ref[...], gathered_ref[:, : gathered_ref.shape[1] - model_width], TN).astype(out_ref.dtype)
    head_width = d_head.shape[1]
    lanes = width - head_width
    for shard in range(shards):
        for group in range(groups):
            first = (group * shards + shard) * own_rows
            out_ref[shard, group, :, :head_width] = attend[first : first + own_rows]
            piece = expand[shard * own_rows : (shard + 1) * own_rows, group * lanes : (group + 1) * lanes]
            out_ref[shard, group, :, head_width:] = piece


def head_grads(gathered, d_query, d_kv, attended, model_width, groups, shards):
    width = 3 * d_query.shape[1] + (gathered.shape[1] - model_width) // groups
    vmem = pl.BlockSpec(memory_space=pltpu.VMEM)
    return pl.pallas_call(
        head_grads_body,
        out_shape=jax.ShapeDtypeStruct((shards, groups, model_width // groups // shards, width), jnp.bfloat16),
        in_specs=[vmem] * 4,
        out_specs=vmem,
        compiler_params=pltpu.CompilerParams(vmem_limit_bytes=24 * 1024 * 1024),
        name="head_grads",
    )(gathered, d_query, d_kv, attended)


def short_grads_body(shards, *refs):
    grouped_refs, cols_refs, out_ref = refs[:shards], refs[shards : 2 * shards], refs[-1]
    count, tall, lanes = out_ref.shape
    grouped = jnp.concatenate([ref[...] for ref in grouped_refs], axis=0)
    cols = jnp.concatenate([ref[...] for ref in cols_refs], axis=0)
    short = mm(grouped, cols, TN).astype(jnp.bfloat16)
    parts = short.shape[1] // lanes
    own_rows = tall // parts
    for part in range(parts):
        piece = short[:, part * lanes : (part + 1) * lanes].reshape(count, own_rows, lanes)
        out_ref[:, part * own_rows : (part + 1) * own_rows, :] = piece


def short_grads(grouped, cols, count, lanes):
    tall = grouped[0].shape[1] // count * (cols[0].shape[1] // lanes)
    vmem = pl.BlockSpec(memory_space=pltpu.VMEM)
    return pl.pallas_call(
        functools.partial(short_grads_body, len(grouped)),
        out_shape=jax.ShapeDtypeStruct((count, tall, lanes), jnp.bfloat16),
        in_specs=[vmem] * (2 * len(grouped)),
        out_specs=vmem,
        name="short_grads",
    )(*grouped, *cols)


def assemble_heads_body(parts_ref, came_ref, expand_ref, attend_ref):
    heads, _, width = parts_ref.shape
    lanes = expand_ref.shape[1] // heads
    head_lanes = attend_ref.shape[1] // 3 // heads
    for head in range(heads):
        expand_ref[:, head * lanes : (head + 1) * lanes] = parts_ref[head, :, width - lanes :].astype(jnp.float32)
        for part in range(3):
            first = (part * heads + head) * head_lanes
            piece = came_ref[head, :, part * head_lanes : (part + 1) * head_lanes]
            attend_ref[:, first : first + head_lanes] = piece.astype(jnp.float32)


def assemble_heads(parts, came, expand_width, qkv_width):
    own_rows = parts.shape[1]
    vmem = pl.BlockSpec(memory_space=pltpu.VMEM)
    return pl.pallas_call(
        assemble_heads_body,
        out_shape=[
            jax.ShapeDtypeStruct((own_rows, expand_width), jnp.float32),
            jax.ShapeDtypeStruct((own_rows, qkv_width), jnp.float32),
        ],
        in_specs=[vmem] * 2,
        out_specs=[vmem] * 2,
        name="assemble_heads",
    )(parts, came)


def assemble_short_body(shards, parts_ref, out_ref):
    count, tall, lanes = parts_ref.shape
    own_rows, model_width = out_ref.shape
    parts = tall // own_rows
    for shard in range(shards):
        total = jnp.zeros((tall, lanes), jnp.float32)
        for group in range(count // shards):
            total = total + parts_ref[group * shards + shard].astype(jnp.float32)
        for part in range(parts):
            first = (shard * parts + part) * lanes
            out_ref[:, first : first + lanes] = total[part * own_rows : (part + 1) * own_rows]


def assemble_short(parts, own_rows, model_width, shards):
    vmem = pl.BlockSpec(memory_space=pltpu.VMEM)
    return pl.pallas_call(
        functools.partial(assemble_short_body, shards),
        out_shape=jax.ShapeDtypeStruct((own_rows, model_width), jnp.float32),
        in_specs=[vmem],
        out_specs=vmem,
        name="assemble_short",
    )(parts)


def tie(*values):
    return lax.optimization_barrier(values)


def local(byte_input, w_short, w_attend, w_expand, out_grad):
    z_size, y_size = lax.axis_size("z"), lax.axis_size("y")
    count = z_size * y_size
    short_rows = byte_input.shape[0] // 4
    byte_width = byte_input.shape[1]
    attn_width = w_attend.shape[1] // 3
    model_width = w_short.shape[1]
    head_size = attn_width // HEADS
    both = ("z", "y")
    rows = z_size * short_rows

    def turn_y(value, steps):
        return lax.ppermute(value, "y", [(i, (i + steps) % y_size) for i in range(y_size)])

    def heads_of(*parts):
        stacked = jnp.stack([part.reshape(short_rows, HEADS, head_size) for part in parts], axis=2)
        return stacked.transpose(1, 0, 2, 3).reshape(HEADS, short_rows, len(parts) * head_size)

    def swap(value):
        return lax.all_to_all(value, "z", 0, 0)

    d_expand = out_grad.reshape(short_rows, 4 * byte_width)
    edge = lax.ppermute(byte_input[-3:], both, [(i, i + 1) for i in range(count - 1)])
    d_attended = mm(d_expand, w_expand, NT).astype(jnp.bfloat16)
    grouped = jnp.concatenate([edge, byte_input[:-3]], axis=0).reshape(short_rows, 4 * byte_width)
    hidden = mm(grouped, w_short)
    normed, hidden_scale = unit(hidden)
    normed_b = normed.astype(jnp.bfloat16)
    projected = mm(normed_b, w_attend).astype(jnp.bfloat16)
    key = projected[:, attn_width : 2 * attn_width]
    value = projected[:, 2 * attn_width :]
    kv = swap(heads_of(key, value)).reshape(rows, 2 * head_size)
    qd = heads_of(projected[:, :attn_width], d_attended)
    grouped_y = [grouped] + [turn_y(grouped, step) for step in range(1, y_size)]
    kv, qd, gathered, *grouped_y = tie(kv, qd, jnp.concatenate([d_expand, normed_b], axis=1), *grouped_y)
    gathered = lax.all_gather(gathered, "z", axis=0, tiled=True)
    kvs = [kv] + [turn_y(kv, step) for step in range(1, y_size)]
    qd = swap(qd).reshape(rows, 2 * head_size)
    y = lax.axis_index("y").astype(jnp.int32).reshape(1)
    attended, d_query, own, *sent = attention(y, qd, kvs, short_rows)

    own_rows = model_width // count
    arrived = [turn_y(sent[step - 1], -step) for step in range(1, y_size)]
    total = own
    for part in arrived:
        total = total + part.astype(jnp.float32)
    first_back = jnp.concatenate([attended, d_query], axis=1).reshape(HEADS, short_rows, 2 * head_size)
    first_back = swap(first_back)
    key_unit, key_scale = unit(kv[:, :head_size].astype(jnp.float32))
    d_kv = jnp.concatenate(
        [norm_back(key_unit, key_scale, total[:, :head_size]), total[:, head_size:]], axis=1
    ).astype(jnp.bfloat16)
    first_back, d_kv = tie(first_back, d_kv)
    parts = head_grads(gathered, d_query, d_kv, attended, model_width, z_size, y_size)
    parts, d_kv = tie(parts, d_kv)
    second_back = swap(d_kv.reshape(HEADS, short_rows, 2 * head_size))
    parts = lax.psum_scatter(parts, "y", scatter_dimension=0)
    d_hidden, *d_hidden_y = hidden_grad(y, first_back, second_back, w_attend, normed, hidden_scale, y_size)
    d_hidden_y = d_hidden_y[:1] + [turn_y(d_hidden_y[step], step) for step in range(1, y_size)]
    parts, d_hidden = tie(parts, d_hidden)
    d_grouped = mm(d_hidden, w_short, NT).astype(jnp.bfloat16).reshape(4 * short_rows, byte_width)
    *d_hidden_y, d_grouped = tie(*d_hidden_y, d_grouped)
    short = short_grads(grouped_y, d_hidden_y, count, head_size)
    came = swap(parts)
    short, first_back, parts, came = tie(short, first_back, parts, came)
    short = lax.all_to_all(short, both, 0, 0)
    grad_expand, grad_attend = assemble_heads(parts, came, 4 * byte_width, 3 * attn_width)
    attended_own = first_back[:, :, :head_size].transpose(1, 0, 2).reshape(short_rows, attn_width)
    expanded = mm(attended_own, w_expand)
    byte_output = (
        byte_input.astype(jnp.float32) + expanded.reshape(4 * short_rows, byte_width)
    ).astype(jnp.bfloat16)
    back_edge = lax.ppermute(d_grouped[:3], both, [(i + 1, i) for i in range(count - 1)])
    moved = jnp.concatenate([d_grouped[3:], back_edge], axis=0).astype(jnp.float32)
    input_grad = (out_grad.astype(jnp.float32) + moved).astype(jnp.bfloat16)
    short, input_grad, byte_output, grad_attend = tie(short, input_grad, byte_output, grad_attend)
    grad_short = assemble_short(short, own_rows, model_width, y_size)
    return (byte_output, input_grad, grad_short, grad_attend, grad_expand)


def solution(mesh):
    docs, seq = mesh.devices.shape
    fine = Mesh(mesh.devices.reshape(docs, HEADS, seq // HEADS), ("docs", "z", "y"))
    split = P(("docs", "z", "y"), None)
    return jax.shard_map(
        local, mesh=fine, in_specs=(split, P(), P(), P(), split), out_specs=(split,) * 5, check_vma=False
    )
```

```python
import functools

import jax
import jax.numpy as jnp
from jax import lax
from jax.experimental import pallas as pl
from jax.experimental.pallas import tpu as pltpu
from jax.sharding import Mesh, PartitionSpec as P

HEADS = 8


SCORE_BOUND = 16.0
EPSILON = 1e-06

NT = (((1,), (1,)), ((), ()))
TN = (((0,), (0,)), ((), ()))


def mm(left, right, dims=(((1,), (0,)), ((), ()))):
    return lax.dot_general(left, right, dims, preferred_element_type=jnp.float32)


def unit(matrix):
    scale = lax.rsqrt(jnp.mean(matrix * matrix, axis=1, keepdims=True) + EPSILON)
    return (matrix * scale, scale)


def norm_back(normed, scale, upstream):
    inner = jnp.mean(normed * upstream, axis=1, keepdims=True)
    return scale * (upstream - normed * inner)


def chunks_of(rows, block, width=256):
    found = []
    for first in range(0, rows, width):
        found.append((first, min(width, rows - first), first // block * block))
    return found


def attention_body(block, shards, y_ref, qd_ref, *refs):
    kv_refs = refs[:shards]
    att_ref, dq_ref, own_ref = refs[shards : shards + 3]
    sent_refs = refs[shards + 3 : 2 * shards + 2]
    p_ref, kb_ref, acc_ref, dq_acc = refs[2 * shards + 2 :]
    rows, head_size = att_ref.shape
    factor = SCORE_BOUND / head_size
    chunks = chunks_of(rows, block)
    y = y_ref[0]
    query_unit, query_scale = unit(qd_ref[:, :head_size].astype(jnp.float32))
    qb = query_unit.astype(jnp.bfloat16)
    qpos = lax.broadcasted_iota(jnp.int32, (rows, 1), 0)
    start = jnp.zeros((rows, 1), jnp.int32)
    for edge in range(block, rows, block):
        start = start + jnp.where(qpos >= edge, block, 0)
    denom = jnp.zeros((rows, 1), jnp.float32)
    acc_ref[...] = jnp.zeros_like(acc_ref)
    for turn in range(shards):
        key_unit, _ = unit(kv_refs[turn][:, :head_size].astype(jnp.float32))
        kb_ref[turn] = key_unit.astype(jnp.bfloat16)
        limit = qpos + 1 if turn == 0 else start + jnp.where(y >= turn, block, 0)
        for number, (first, width, row) in enumerate(chunks):
            dots = mm(qb[row:], kb_ref[turn, first : first + width], NT)
            key_pos = first + lax.broadcasted_iota(jnp.int32, (rows - row, width), 1)
            powers = jnp.where(key_pos < limit[row:], jnp.exp(dots * factor), 0.0)
            p_ref[turn, number, row:, :width] = powers
            part = jnp.sum(powers, axis=1, keepdims=True)
            denom = denom + (part if row == 0 else jnp.concatenate([jnp.zeros((row, 1), jnp.float32), part], axis=0))
            acc_ref[row:] += mm(powers.astype(jnp.bfloat16), kv_refs[turn][first : first + width, head_size:])
    inverse = 1.0 / denom
    attended = (acc_ref[...] * inverse).astype(jnp.bfloat16)
    att_ref[...] = attended
    d_attended = qd_ref[:, head_size:].astype(jnp.float32)
    grad = (d_attended * inverse).astype(jnp.bfloat16)
    shift = jnp.sum(d_attended * attended.astype(jnp.float32), axis=1, keepdims=True) * inverse
    shift = shift.astype(jnp.bfloat16).astype(jnp.float32)
    dq_acc[...] = jnp.zeros_like(dq_acc)
    for turn in range(shards):
        out = own_ref if turn == 0 else sent_refs[turn - 1]
        for number, (first, width, row) in enumerate(chunks):
            powers = p_ref[turn, number, row:, :width]
            grad_dot = mm(grad[row:], kv_refs[turn][first : first + width, head_size:], NT)
            d_score = (powers * (grad_dot - shift[row:]) * factor).astype(jnp.bfloat16)
            dq_acc[row:] += mm(d_score, kb_ref[turn, first : first + width])
            out[first : first + width, :head_size] = mm(d_score, qb[row:], TN).astype(out.dtype)
            out[first : first + width, head_size:] = mm(powers.astype(jnp.bfloat16), grad[row:], TN).astype(out.dtype)
    dq_ref[...] = norm_back(query_unit, query_scale, dq_acc[...]).astype(jnp.bfloat16)


def attention(y, qd, kvs, block):
    rows, width = qd.shape
    head_size = width // 2
    shards = len(kvs)
    vmem = pl.BlockSpec(memory_space=pltpu.VMEM)
    shape = jax.ShapeDtypeStruct
    outs = [shape((rows, head_size), jnp.bfloat16)] * 2
    outs += [shape((rows, width), jnp.float32)] + [shape((rows, width), jnp.bfloat16)] * (shards - 1)
    return pl.pallas_call(
        functools.partial(attention_body, block, shards),
        out_shape=outs,
        in_specs=[pl.BlockSpec(memory_space=pltpu.SMEM)] + [vmem] * (shards + 1),
        out_specs=[vmem] * len(outs),
        scratch_shapes=[
            pltpu.VMEM((shards, len(chunks_of(rows, block)), rows, 256), jnp.float32),
            pltpu.VMEM((shards, rows, head_size), jnp.bfloat16),
            pltpu.VMEM((rows, head_size), jnp.float32),
            pltpu.VMEM((rows, head_size), jnp.float32),
        ],
        compiler_params=pltpu.CompilerParams(vmem_limit_bytes=40 * 1024 * 1024),
        name="attention",
    )(y, qd, *kvs)


def hidden_grad_body(y_ref, first_ref, second_ref, weight_ref, normed_ref, scale_ref, out_ref, *refs):
    cols_refs, (joined_ref,) = refs[:-1], refs[-1:]
    heads, rows, width = first_ref.shape
    lanes = width // 2
    attn_width = heads * lanes
    for head in range(heads):
        places = [part * attn_width + head * lanes for part in range(3)]
        joined_ref[:, places[0] : places[0] + lanes] = first_ref[head, :, lanes:]
        joined_ref[:, places[1] : places[1] + lanes] = second_ref[head, :, :lanes]
        joined_ref[:, places[2] : places[2] + lanes] = second_ref[head, :, lanes:]
    d_normed = mm(joined_ref[...], weight_ref[...], NT)
    out_ref[...] = norm_back(normed_ref[...], scale_ref[...], d_normed).astype(jnp.bfloat16)
    count = len(cols_refs)
    y_cols = out_ref.shape[1] // count
    for step, cols_ref in enumerate(cols_refs):
        first = pl.multiple_of(lax.rem(y_ref[0] + step, count) * y_cols, y_cols)
        cols_ref[...] = out_ref[:, pl.ds(first, y_cols)]


def hidden_grad(y, first, second, weight, normed, scale, y_size):
    rows, model_width = normed.shape
    vmem = pl.BlockSpec(memory_space=pltpu.VMEM)
    outs = [jax.ShapeDtypeStruct((rows, model_width), jnp.bfloat16)]
    outs += [jax.ShapeDtypeStruct((rows, model_width // y_size), jnp.bfloat16)] * y_size
    return pl.pallas_call(
        hidden_grad_body,
        out_shape=outs,
        in_specs=[pl.BlockSpec(memory_space=pltpu.SMEM)] + [vmem] * 5,
        out_specs=[vmem] * len(outs),
        scratch_shapes=[pltpu.VMEM((rows, weight.shape[1]), jnp.bfloat16)],
        compiler_params=pltpu.CompilerParams(vmem_limit_bytes=24 * 1024 * 1024),
        name="hidden_grad",
    )(y, first, second, weight, normed, scale)


def head_grads_body(gathered_ref, dq_ref, dkv_ref, attended_ref, out_ref):
    shards, groups, own_rows, width = out_ref.shape
    model_width = groups * shards * own_rows
    d_head = jnp.concatenate([dq_ref[...], dkv_ref[...]], axis=1)
    attend = mm(gathered_ref[:, gathered_ref.shape[1] - model_width :], d_head, TN).astype(out_ref.dtype)
    expand = mm(attended_ref[...], gathered_ref[:, : gathered_ref.shape[1] - model_width], TN).astype(out_ref.dtype)
    head_width = d_head.shape[1]
    lanes = width - head_width
    for shard in range(shards):
        for group in range(groups):
            first = (group * shards + shard) * own_rows
            out_ref[shard, group, :, :head_width] = attend[first : first + own_rows]
            piece = expand[shard * own_rows : (shard + 1) * own_rows, group * lanes : (group + 1) * lanes]
            out_ref[shard, group, :, head_width:] = piece


def head_grads(gathered, d_query, d_kv, attended, model_width, groups, shards):
    width = 3 * d_query.shape[1] + (gathered.shape[1] - model_width) // groups
    vmem = pl.BlockSpec(memory_space=pltpu.VMEM)
    return pl.pallas_call(
        head_grads_body,
        out_shape=jax.ShapeDtypeStruct((shards, groups, model_width // groups // shards, width), jnp.bfloat16),
        in_specs=[vmem] * 4,
        out_specs=vmem,
        compiler_params=pltpu.CompilerParams(vmem_limit_bytes=24 * 1024 * 1024),
        name="head_grads",
    )(gathered, d_query, d_kv, attended)


def split_parts_body(z_ref, parts_ref, expand_ref, *piece_refs):
    groups, _, width = parts_ref.shape
    head_width = piece_refs[0].shape[1]
    lanes = width - head_width
    for group in range(groups):
        expand_ref[:, group * lanes : (group + 1) * lanes] = parts_ref[group, :, head_width:].astype(jnp.float32)
    for step, piece_ref in enumerate(piece_refs):
        piece_ref[...] = parts_ref[lax.rem(z_ref[0] + step, groups), :, :head_width]


def split_parts(z, parts, head_width):
    groups, own_rows, width = parts.shape
    vmem = pl.BlockSpec(memory_space=pltpu.VMEM)
    outs = [jax.ShapeDtypeStruct((own_rows, (width - head_width) * groups), jnp.float32)]
    outs += [jax.ShapeDtypeStruct((own_rows, head_width), jnp.bfloat16)] * groups
    return pl.pallas_call(
        split_parts_body,
        out_shape=outs,
        in_specs=[pl.BlockSpec(memory_space=pltpu.SMEM), vmem],
        out_specs=[vmem] * len(outs),
        name="split_parts",
    )(z, parts)


def short_grads_body(shards, *refs):
    grouped_refs, cols_refs, out_ref = refs[:shards], refs[shards : 2 * shards], refs[-1]
    count, tall, lanes = out_ref.shape
    grouped = jnp.concatenate([ref[...] for ref in grouped_refs], axis=0)
    cols = jnp.concatenate([ref[...] for ref in cols_refs], axis=0)
    short = mm(grouped, cols, TN).astype(jnp.bfloat16)
    parts = short.shape[1] // lanes
    own_rows = tall // parts
    for part in range(parts):
        piece = short[:, part * lanes : (part + 1) * lanes].reshape(count, own_rows, lanes)
        out_ref[:, part * own_rows : (part + 1) * own_rows, :] = piece


def short_grads(grouped, cols, count, lanes):
    tall = grouped[0].shape[1] // count * (cols[0].shape[1] // lanes)
    vmem = pl.BlockSpec(memory_space=pltpu.VMEM)
    return pl.pallas_call(
        functools.partial(short_grads_body, len(grouped)),
        out_shape=jax.ShapeDtypeStruct((count, tall, lanes), jnp.bfloat16),
        in_specs=[vmem] * (2 * len(grouped)),
        out_specs=vmem,
        name="short_grads",
    )(*grouped, *cols)


def assemble_attend_body(z_ref, *refs):
    piece_refs, out_ref = refs[:-1], refs[-1]
    groups = len(piece_refs)
    lanes = piece_refs[0].shape[1] // 3
    for step, piece_ref in enumerate(piece_refs):
        head = lax.rem(z_ref[0] + (groups - step), groups)
        for part in range(3):
            first = pl.multiple_of((part * groups + head) * lanes, lanes)
            piece = piece_ref[:, part * lanes : (part + 1) * lanes].astype(jnp.float32)
            out_ref[:, pl.ds(first, lanes)] = piece


def assemble_attend(z, pieces):
    own_rows, width = pieces[0].shape
    vmem = pl.BlockSpec(memory_space=pltpu.VMEM)
    return pl.pallas_call(
        assemble_attend_body,
        out_shape=jax.ShapeDtypeStruct((own_rows, width * len(pieces)), jnp.float32),
        in_specs=[pl.BlockSpec(memory_space=pltpu.SMEM)] + [vmem] * len(pieces),
        out_specs=vmem,
        name="assemble_attend",
    )(z, *pieces)


def assemble_short_body(shards, parts_ref, out_ref):
    count, tall, lanes = parts_ref.shape
    own_rows, model_width = out_ref.shape
    parts = tall // own_rows
    for shard in range(shards):
        total = jnp.zeros((tall, lanes), jnp.float32)
        for group in range(count // shards):
            total = total + parts_ref[group * shards + shard].astype(jnp.float32)
        for part in range(parts):
            first = (shard * parts + part) * lanes
            out_ref[:, first : first + lanes] = total[part * own_rows : (part + 1) * own_rows]


def assemble_short(parts, own_rows, model_width, shards):
    vmem = pl.BlockSpec(memory_space=pltpu.VMEM)
    return pl.pallas_call(
        functools.partial(assemble_short_body, shards),
        out_shape=jax.ShapeDtypeStruct((own_rows, model_width), jnp.float32),
        in_specs=[vmem],
        out_specs=vmem,
        name="assemble_short",
    )(parts)


def tie(*values):
    return lax.optimization_barrier(values)


def local(byte_input, w_short, w_attend, w_expand, out_grad):
    z_size, y_size = lax.axis_size("z"), lax.axis_size("y")
    count = z_size * y_size
    short_rows = byte_input.shape[0] // 4
    byte_width = byte_input.shape[1]
    attn_width = w_attend.shape[1] // 3
    model_width = w_short.shape[1]
    head_size = attn_width // HEADS
    both = ("z", "y")
    rows = z_size * short_rows

    def turn_y(value, steps):
        return lax.ppermute(value, "y", [(i, (i + steps) % y_size) for i in range(y_size)])

    def heads_of(*parts):
        stacked = jnp.stack([part.reshape(short_rows, HEADS, head_size) for part in parts], axis=2)
        return stacked.transpose(1, 0, 2, 3).reshape(HEADS, short_rows, len(parts) * head_size)

    def swap(value):
        return lax.all_to_all(value, "z", 0, 0)

    d_expand = out_grad.reshape(short_rows, 4 * byte_width)
    edge = lax.ppermute(byte_input[-3:], both, [(i, i + 1) for i in range(count - 1)])
    d_attended = mm(d_expand, w_expand, NT).astype(jnp.bfloat16)
    grouped = jnp.concatenate([edge, byte_input[:-3]], axis=0).reshape(short_rows, 4 * byte_width)
    hidden = mm(grouped, w_short)
    normed, hidden_scale = unit(hidden)
    normed_b = normed.astype(jnp.bfloat16)
    projected = mm(normed_b, w_attend).astype(jnp.bfloat16)
    key = projected[:, attn_width : 2 * attn_width]
    value = projected[:, 2 * attn_width :]
    kv = swap(heads_of(key, value)).reshape(rows, 2 * head_size)
    qd = heads_of(projected[:, :attn_width], d_attended)
    grouped_y = [grouped] + [turn_y(grouped, step) for step in range(1, y_size)]
    kv, qd, gathered, *grouped_y = tie(kv, qd, jnp.concatenate([d_expand, normed_b], axis=1), *grouped_y)
    gathered = lax.all_gather(gathered, "z", axis=0, tiled=True)
    kvs = [kv] + [turn_y(kv, step) for step in range(1, y_size)]
    qd = swap(qd).reshape(rows, 2 * head_size)
    y = lax.axis_index("y").astype(jnp.int32).reshape(1)
    attended, d_query, own, *sent = attention(y, qd, kvs, short_rows)

    own_rows = model_width // count
    arrived = [turn_y(sent[step - 1], -step) for step in range(1, y_size)]
    total = own
    for part in arrived:
        total = total + part.astype(jnp.float32)
    first_back = jnp.concatenate([attended, d_query], axis=1).reshape(HEADS, short_rows, 2 * head_size)
    first_back = swap(first_back)
    key_unit, key_scale = unit(kv[:, :head_size].astype(jnp.float32))
    d_kv = jnp.concatenate(
        [norm_back(key_unit, key_scale, total[:, :head_size]), total[:, head_size:]], axis=1
    ).astype(jnp.bfloat16)
    first_back, d_kv = tie(first_back, d_kv)
    parts = head_grads(gathered, d_query, d_kv, attended, model_width, z_size, y_size)
    second_back = swap(d_kv.reshape(HEADS, short_rows, 2 * head_size))
    second_back, parts = tie(second_back, parts)
    parts = lax.psum_scatter(parts, "y", scatter_dimension=0)
    d_hidden, *d_hidden_y = hidden_grad(y, first_back, second_back, w_attend, normed, hidden_scale, y_size)
    d_hidden_y = d_hidden_y[:1] + [turn_y(d_hidden_y[step], step) for step in range(1, y_size)]
    d_grouped = mm(d_hidden, w_short, NT).astype(jnp.bfloat16).reshape(4 * short_rows, byte_width)
    *d_hidden_y, d_grouped = tie(*d_hidden_y, d_grouped)
    short = short_grads(grouped_y, d_hidden_y, count, head_size)
    short, first_back = tie(short, first_back)
    short = lax.all_to_all(short, both, 0, 0)
    z = lax.axis_index("z").astype(jnp.int32).reshape(1)
    grad_expand, *pieces = split_parts(z, parts, 3 * head_size)
    pieces = pieces[:1] + [
        lax.ppermute(pieces[step], "z", [(i, (i + step) % z_size) for i in range(z_size)])
        for step in range(1, z_size)
    ]
    grad_attend = assemble_attend(z, pieces)
    attended_own = first_back[:, :, :head_size].transpose(1, 0, 2).reshape(short_rows, attn_width)
    expanded = mm(attended_own, w_expand)
    byte_output = (
        byte_input.astype(jnp.float32) + expanded.reshape(4 * short_rows, byte_width)
    ).astype(jnp.bfloat16)
    back_edge = lax.ppermute(d_grouped[:3], both, [(i + 1, i) for i in range(count - 1)])
    moved = jnp.concatenate([d_grouped[3:], back_edge], axis=0).astype(jnp.float32)
    input_grad = (out_grad.astype(jnp.float32) + moved).astype(jnp.bfloat16)
    short, input_grad, byte_output, grad_attend = tie(short, input_grad, byte_output, grad_attend)
    grad_short = assemble_short(short, own_rows, model_width, y_size)
    return (byte_output, input_grad, grad_short, grad_attend, grad_expand)


def solution(mesh):
    docs, seq = mesh.devices.shape
    fine = Mesh(mesh.devices.reshape(docs, HEADS, seq // HEADS), ("docs", "z", "y"))
    split = P(("docs", "z", "y"), None)
    return jax.shard_map(
        local, mesh=fine, in_specs=(split, P(), P(), P(), split), out_specs=(split,) * 5, check_vma=False
    )
```
